256 devices in a mesh: seq: 32 (over x_hi, z, core), ch: 8 (over y, x_lo).
Axes of the slice: x: 4 (x_hi: 2, x_lo: 2; x = x_hi * 2 + x_lo), y: 4, z: 8, core: 2. Of those that a mesh axis runs over, the one named last changes fastest.
Arguments:
- hidden: bfloat16 [4096, 2048], P('seq', 'ch'), may hold values from -400 to 400, as said below
- tokens: int32 [4096], replicated, may hold values from 0 to 3
- edit_bounds: int32 [8, 2], replicated, may hold values from 0 to 4095
- norm_gain: float32 [2048], replicated, may hold values from 0.1 to 1.9
- base_embed: float32 [4, 2048], replicated, may hold values from -6 to 6
- w_in: bfloat16 [2, 2048, 4096], P(None, None, 'ch'), may hold values from -0.125 to 0.125
- conv_w: float32 [4, 4096], P(None, 'ch'), may hold values from -3 to 3
- conv_b: float32 [4096], P('ch'), may hold values from -3 to 3
- proj_bc: bfloat16 [32, 4096], P(None, 'ch'), may hold values from -0.1875 to 0.1875
- decay_rate: float32 [16, 4096], P(None, 'ch'), may hold values from 9.765625e-06 to 0.11, as said below
- skip_gain: float32 [4096], P('ch'), may hold values from -4 to 4
- w_out: bfloat16 [4096, 2048], P('ch'), may hold values from -0.09375 to 0.09375
Outputs:
- mixed: bfloat16 [4096, 2048], P('seq', 'ch')
The draws below stay inside these ranges and needn't reach their ends.
Inputs may be any that keep to these rules, and one draw needn't show every extreme that they name: The hidden states have row and column scales that differ. `decay_rate`: each entry is a positive decay rate per position. `edit_bounds`: positions in the window; a span's start and end come in no fixed order and may coincide with others.
All inputs are finite; a program needn't handle non-finite values.
Results may differ from the reference program's by a relative error of at most 0.014.
Values may be sent and summed in bfloat16 or wider, within the bound.
A program may use at most 64 MiB of HBM per device.

```python
import math
import jax
import jax.numpy as jnp
from jax import lax

D = 2048
E = 4096
N = 16
CONV = 4
SPANS = 8
L_DEV = 128
TOTAL = 4096


def draw_hidden(key, part):
    first_key, second_key, third_key = jax.random.split(key, 3)
    base_values = jax.random.truncated_normal(first_key, -4.0, 4.0, (TOTAL, D), jnp.float32)
    row_scale = jnp.exp(jax.random.uniform(second_key, (TOTAL, 1), jnp.float32, 0.0, math.log(10.0)))
    column_scale = jnp.exp(jax.random.uniform(third_key, (1, D), jnp.float32, 0.0, math.log(10.0)))
    return (base_values * row_scale * column_scale).astype(jnp.bfloat16)


def draw_decay_rate(key, part):
    first_key, second_key, third_key = jax.random.split(key, 3)
    slow_share = 0.5
    slow_pick = jax.random.uniform(first_key, (N, E), jnp.float32) < slow_share
    slow_rate = jnp.exp(jax.random.uniform(second_key, (N, E), jnp.float32, math.log(0.05 / TOTAL), math.log(1.0 / TOTAL)))
    fast_rate = jnp.exp(jax.random.uniform(third_key, (N, E), jnp.float32, math.log(1.0 / 50.0), math.log(0.1)))
    return jnp.where(slow_pick, slow_rate, fast_rate)


def plant(values, stream_key, low, high):
    longest = values.shape.index(max(values.shape))
    spots = []
    for shift in (0, 1):
        where = [jax.random.randint(jax.random.fold_in(stream_key, axis), (), 0, length) for axis, length in enumerate(values.shape)]
        where[longest] = (where[longest] + shift) % values.shape[longest]
        spots.append(tuple(where))
    return values.at[spots[0]].set(low).at[spots[1]].set(high)


def block_scale(rng, dims, shards, low, top_value):
    loudness, own = 1.0, jax.random.fold_in(rng, 6)
    for dim, shards_of in shards:
        heights = jnp.exp(jax.random.uniform(jax.random.fold_in(own, dim), (shards_of,), jnp.float32, low / len(shards), top_value / len(shards)))
        loudness = loudness * jnp.repeat(heights, dims[dim] // shards_of).reshape([-1 if axis == dim else 1 for axis in range(len(dims))])
    return loudness


def scatter_about(stream_key, extent, scale, bound, pieces=(), kind=jnp.bfloat16):
    result = jax.random.normal(stream_key, extent, jnp.float32) * scale
    if len(pieces) > 0:
        result = block_scale(stream_key, extent, pieces, -0.22, 0.18) * result
    return jnp.clip(result, min=-bound, max=bound).astype(kind)


def setup_inputs(seed: int = 0) -> dict:
    arg_keys = jax.random.split(jax.random.key(seed), 13)
    hidden = draw_hidden(jax.random.fold_in(arg_keys[12], 71), 0)
    tokens = plant(jax.random.randint(arg_keys[1], (TOTAL,), 0, 4), jax.random.fold_in(arg_keys[1], 1), 0, 3).astype(jnp.int32)
    edit_bounds = plant(jax.random.randint(arg_keys[2], (SPANS, 2), 0, TOTAL), jax.random.fold_in(arg_keys[2], 1), 0, TOTAL - 1).astype(jnp.int32)
    norm_gain = jnp.clip(1.0 + 0.18 * jax.random.normal(arg_keys[3], (D,), jnp.float32), 0.1, 1.9)
    base_embed = scatter_about(arg_keys[4], (4, D), 1.0, 6.0, (), jnp.float32)
    w_in = scatter_about(arg_keys[5], (2, D, E), D ** -0.5, 0.125, ((2, 8),))
    conv_w = scatter_about(arg_keys[6], (CONV, E), CONV ** -0.5, 3.0, ((1, 8),), jnp.float32)
    conv_b = scatter_about(arg_keys[7], (E,), 0.5, 3.0, ((0, 8),), jnp.float32)
    proj_bc = scatter_about(arg_keys[8], (2 * N, E), (E // 4) ** -0.5, 0.1875, ((1, 8),))
    decay_rate = draw_decay_rate(jax.random.fold_in(arg_keys[12], 71), 0)
    skip_gain = scatter_about(arg_keys[10], (E,), 1.0, 4.0, ((0, 8),), jnp.float32)
    w_out = scatter_about(arg_keys[11], (E, D), E ** -0.5, 0.09375, ((0, 8),))
    return dict(hidden=hidden, tokens=tokens, edit_bounds=edit_bounds, norm_gain=norm_gain, base_embed=base_embed, w_in=w_in, conv_w=conv_w, conv_b=conv_b, proj_bc=proj_bc, decay_rate=decay_rate, skip_gain=skip_gain, w_out=w_out)


epsilon = 1e-05

def link(before, follow):
    return (before[0] * follow[0], before[1] * follow[0] + follow[1])

def run_stream(row_block, keep_rate, w_in, conv_w, conv_b, proj_bc, decay_rate, skip_gain):
    x_part = jnp.dot(row_block, w_in[0], preferred_element_type=jnp.float32).astype(jnp.bfloat16)
    z_part = jnp.dot(row_block, w_in[1], preferred_element_type=jnp.float32).astype(jnp.bfloat16)
    inner_width = x_part.shape[1]
    padded = jnp.concatenate([jnp.zeros((CONV - 1, inner_width), jnp.bfloat16), x_part], axis=0)
    conv_sum = conv_b[None, :] + jnp.zeros((TOTAL, inner_width), jnp.float32)
    for tap_index in range(CONV):
        conv_sum = conv_sum + padded[tap_index:tap_index + TOTAL].astype(jnp.float32) * conv_w[tap_index][None, :]
    mixed_in = jax.nn.silu(conv_sum).astype(jnp.bfloat16)
    inputs_bc = jnp.dot(proj_bc, mixed_in.T, preferred_element_type=jnp.float32)
    decay_mult = jnp.exp(-decay_rate)
    drive_gain = jnp.sqrt(-jnp.expm1(-2.0 * decay_rate))
    blocks = TOTAL // L_DEV
    block_inputs = (keep_rate.reshape(blocks, L_DEV), inputs_bc[:N].reshape(N, blocks, L_DEV).transpose(1, 0, 2), inputs_bc[N:].reshape(N, blocks, L_DEV).transpose(1, 0, 2), mixed_in.reshape(blocks, L_DEV, inner_width))

    def block_step(carry_in, block):
        keep_block, state_in, state_out, x_block = block
        x_float = x_block.astype(jnp.float32)
        decay_rows = keep_block[:, None, None] * decay_mult[None]
        drive_terms = drive_gain[None] * state_in.T[:, :, None] * x_float[:, None, :]
        cum_decay, local_state = lax.associative_scan(link, (decay_rows, drive_terms), axis=0)
        full_state = local_state + cum_decay * carry_in[None]
        y_out = jnp.einsum('nl,lne->le', state_out, full_state) + skip_gain[None] * x_float
        return (full_state[-1], y_out)
    zero_state = jnp.zeros((N, inner_width), jnp.float32)
    final_state, block_outputs = lax.scan(block_step, zero_state, block_inputs)
    y_all = block_outputs.reshape(TOTAL, inner_width)
    return (y_all * jax.nn.silu(z_part.astype(jnp.float32))).astype(jnp.bfloat16)

def reference(hidden, tokens, edit_bounds, norm_gain, base_embed, w_in, conv_w, conv_b, proj_bc, decay_rate, skip_gain, w_out):
    row_values = hidden.astype(jnp.float32)
    inv_rms = lax.rsqrt(lax.optimization_barrier(jnp.mean(row_values * row_values, axis=1, keepdims=True)) + epsilon)
    one_hot = (tokens[:, None] == jnp.arange(4, dtype=jnp.int32)[None, :]).astype(jnp.float32)
    embedded = one_hot[:, 0:1] * base_embed[0][None, :]
    for base_index in range(1, 4):
        embedded = embedded + one_hot[:, base_index:base_index + 1] * base_embed[base_index][None, :]
    normed = (row_values * inv_rms * norm_gain[None, :] + embedded).astype(jnp.bfloat16)
    places = jnp.arange(TOTAL, dtype=jnp.int32)
    hit_count = lax.optimization_barrier(jnp.sum((places[:, None] == edit_bounds.reshape(-1)[None, :]).astype(jnp.float32), axis=1))
    keep_rate = 1.0 / (1.0 + hit_count)
    forward_out = run_stream(normed, keep_rate, w_in, conv_w, conv_b, proj_bc, decay_rate, skip_gain)
    backward_out = run_stream(normed[::-1, ::-1], keep_rate[::-1], w_in, conv_w, conv_b, proj_bc, decay_rate, skip_gain)[::-1]
    summed = jnp.dot(forward_out, w_out, preferred_element_type=jnp.float32) + jnp.dot(backward_out, w_out, preferred_element_type=jnp.float32)[:, ::-1]
    return summed.astype(jnp.bfloat16)
```

```python
import functools

import jax
import jax.numpy as jnp
from jax import lax
from jax.experimental import pallas as pl
from jax.experimental.pallas import tpu as pltpu
from jax.sharding import PartitionSpec as P

MESH = pl.DeviceIdType.MESH
F32 = jnp.float32
BF16 = jnp.bfloat16
CONV = 4
EPSILON = 1e-05
HALO = 8
SUB = 8
LANES = 128
PER_TURN = 16


def exchange(width, dtype):
    row = lax.broadcasted_iota(jnp.int32, (width, width), 0)
    col = lax.broadcasted_iota(jnp.int32, (width, width), 1)
    return (row + col == width - 1).astype(F32).astype(dtype)


def one_minus_exp(x):
    series = jnp.ones_like(x)
    for order in range(11, 1, -1):
        series = 1.0 - series * x * (1.0 / order)
    return jnp.where(x < 0.5, series * x, 1.0 - jnp.exp(-x))


def silu(x):
    return x * jax.nn.sigmoid(x)


def layer_kernel(
    S, C, L, N,
    tokens_h, bounds, hidden_h, gain_h, embed_h, w_in_h, conv_w_h, conv_b_h, proj_h, rate_h, skip_h, w_out_h,
    out_ref,
    tokens, gain, embed, w_in, conv_w, conv_b, proj, rate, skip, w_cat,
    rows_in, prev_in, next_in, normed,
    x_fore, x_back, z_gate, c_tiles, y_tiles,
    bc_send, bc_recv, b_tiles, r_tiles, a_tiles, g_tiles, block_keep,
    end_send, end_recv, start_send, start_recv,
    y_both, out_send, out_recv,
    local_sem, gather_s, gather_r, prev_s, prev_r, next_s, next_r,
    bc_s, bc_r, end_s, end_r, start_s, start_r, out_s, out_r,
):
    seq = lax.axis_index("seq")
    ch = lax.axis_index("ch")
    halves = 2
    Q = S // halves
    per_owner = N // Q
    half = seq // Q
    own_slot = lax.rem(seq, Q)
    width = hidden_h.shape[1]
    inner = w_in.shape[2]
    chunks = inner // LANES

    def at_seq(offset):
        return lax.rem(seq + offset + S, S)

    def at_ch(offset):
        return lax.rem(ch + offset + C, C)

    fetched = [
        (tokens_h, tokens), (gain_h, gain), (embed_h, embed), (conv_w_h, conv_w), (conv_b_h, conv_b),
        (proj_h, proj), (rate_h, rate), (skip_h, skip), (hidden_h, rows_in.at[ch]),
        (w_in_h.at[0], w_in.at[0]), (w_in_h.at[1], w_in.at[1]),
    ]
    fetched += [
        (w_out_h.at[:, pl.ds(k * width, width)], w_cat.at[k, pl.ds(0, inner)]) for k in range(C)
    ]
    local = [
        pltpu.make_async_copy(src, dst, local_sem.at[k]) for k, (src, dst) in enumerate(fetched)
    ]
    for copy in local:
        copy.start()

    barrier = pltpu.get_barrier_semaphore()
    partners = [(seq, at_ch(d)) for d in range(1, C)]
    partners += [(at_seq(side), at_ch(d)) for side in (1, -1) for d in range(C)]
    partners += [(at_seq(d), ch) for d in range(2, S - 1)]
    for partner in partners:
        pl.semaphore_signal(barrier, inc=1, device_id=partner, device_id_type=MESH)
    pl.semaphore_wait(barrier, len(partners))

    def send(src, dst, send_sem, recv_sem, where):
        copy = pltpu.make_async_remote_copy(
            src_ref=src, dst_ref=dst, send_sem=send_sem, recv_sem=recv_sem,
            device_id=where, device_id_type=MESH,
        )
        copy.start()
        return copy

    gathers = [
        send(hidden_h, rows_in.at[ch], gather_s.at[d], gather_r.at[d], (seq, at_ch(d)))
        for d in range(1, C)
    ]
    halos = []
    for d in range(C):
        halos.append(
            send(
                hidden_h.at[pl.ds(L - HALO, HALO)], prev_in.at[ch], prev_s.at[d], prev_r.at[d],
                (at_seq(1), at_ch(d)),
            )
        )
        halos.append(
            send(
                hidden_h.at[pl.ds(0, HALO)], next_in.at[ch], next_s.at[d], next_r.at[d],
                (at_seq(-1), at_ch(d)),
            )
        )

    for copy in local:
        copy.wait()

    flip = exchange(width, BF16)
    flip_lanes = exchange(LANES, BF16)
    for k in range(C):
        w_cat[k, pl.ds(inner, inner)] = jnp.dot(
            w_cat[C - 1 - k, pl.ds(0, inner)], flip, preferred_element_type=F32
        ).astype(BF16)
    decay = jnp.exp(-rate[...])
    drive = jnp.sqrt(one_minus_exp(2.0 * rate[...]))
    for k in range(SUB):
        part = slice((k % chunks) * LANES, (k % chunks + 1) * LANES)
        a_tiles[pl.ds(k, N, stride=SUB), :] = decay[:, part]
        g_tiles[pl.ds(k, N, stride=SUB), :] = drive[:, part]

    def keep_at(places):
        hits = jnp.zeros(places.shape, F32)
        for i in range(bounds.shape[0]):
            for j in range(bounds.shape[1]):
                hits = hits + (places == bounds[i, j]).astype(F32)
        return 1.0 / (1.0 + hits)

    lane = lax.broadcasted_iota(jnp.int32, (S, LANES), 1)
    kept = keep_at(lax.broadcasted_iota(jnp.int32, (S, LANES), 0) * L + lane)
    shift = LANES // 2
    while shift:
        kept = kept * pltpu.roll(kept, shift, 1)
        shift //= 2
    block_keep[...] = kept

    lane_row = lax.broadcasted_iota(jnp.int32, (SUB, LANES), 1)

    def running_keep(places):
        run = keep_at(places)
        step = 1
        while step < LANES:
            run = run * jnp.where(lane_row >= step, pltpu.roll(run, step, 1), 1.0)
            step *= 2
        return run[0:1]

    keep_fore = running_keep(seq * L + lane_row)
    keep_back = running_keep(seq * L + (L - 1) - lane_row)

    def base_of(block):
        row = tokens[pl.ds(block, 1), :].astype(F32)
        return jnp.broadcast_to(row, (LANES, LANES)).T[:, 0:1]

    own_base = base_of(seq)
    prev_base = base_of(at_seq(-1))[L - HALO :]
    next_base = base_of(at_seq(1))[:HALO]

    for copy in gathers:
        copy.wait_recv()
    for copy in halos:
        copy.wait_recv()

    def norm_into(block, base, emit):
        total = jnp.zeros((block.shape[1], 1), F32)
        for k in range(C):
            part = block[k].astype(F32)
            total = total + jnp.sum(part * part, axis=1, keepdims=True)
        inv_rms = lax.rsqrt(total * (1.0 / (C * width)) + EPSILON)
        for k in range(C):
            cols = slice(k * width, (k + 1) * width)
            added = jnp.where(base == 0.0, embed[0:1, cols], embed[1:2, cols])
            added = jnp.where(base == 2.0, embed[2:3, cols], added)
            added = jnp.where(base == 3.0, embed[3:4, cols], added)
            emit(k, (block[k].astype(F32) * inv_rms * gain[0:1, cols] + added).astype(BF16))

    def flipped(part):
        return jnp.dot(part, flip, preferred_element_type=F32).astype(BF16)

    def emit_own(k, part):
        normed[0:L, k * width : (k + 1) * width] = part
        k = C - 1 - k
        normed[L : 2 * L, k * width : (k + 1) * width] = flipped(part)

    edge_prev = []
    edge_next = []
    norm_into(rows_in, own_base, emit_own)
    norm_into(prev_in, prev_base, lambda k, part: edge_prev.append(part))
    norm_into(next_in, next_base, lambda k, part: edge_next.append(part))
    for k in range(C):
        both = jnp.concatenate([edge_prev[k], edge_next[k]], axis=0)
        turned = flipped(jnp.concatenate([edge_prev[C - 1 - k], edge_next[C - 1 - k]], axis=0))
        top = lax.broadcasted_iota(jnp.int32, both.shape, 0) < HALO
        normed[2 * L :, k * width : (k + 1) * width] = jnp.where(top, both, turned)

    x_all = jnp.dot(normed[...], w_in[0], preferred_element_type=F32).astype(BF16).astype(F32)
    has_prev = jnp.where(seq > 0, 1.0, 0.0)
    has_next = jnp.where(seq < S - 1, 1.0, 0.0)
    x_fore[0:HALO] = x_all[2 * L : 2 * L + HALO] * has_prev
    x_fore[HALO:] = x_all[0:L]
    x_back[0:L] = x_all[L : 2 * L]
    x_back[L:] = x_all[2 * L + HALO :] * has_next
    sum_fore = jnp.broadcast_to(conv_b[...], (L, inner))
    sum_back = sum_fore
    for k in range(CONV):
        tap = conv_w[k : k + 1, :]
        sum_fore = sum_fore + x_fore[pl.ds(HALO - CONV + 1 + k, L), :] * tap
        sum_back = sum_back + x_back[pl.ds(CONV - 1 - k, L), :] * tap
    c_fore = silu(sum_fore).astype(BF16)
    c_back = silu(sum_back).astype(BF16)

    nt = (((1,), (1,)), ((), ()))
    part_fore = lax.dot_general(proj[...], c_fore, nt, preferred_element_type=F32).astype(BF16)
    part_back = lax.dot_general(proj[...], c_back, nt, preferred_element_type=F32).astype(BF16)
    bc_send[0 : 2 * N] = part_fore
    bc_send[2 * N :] = jnp.dot(part_back, flip_lanes, preferred_element_type=F32).astype(BF16)
    shares = [
        send(bc_send, bc_recv.at[d], bc_s.at[d], bc_r.at[d], (seq, at_ch(d))) for d in range(1, C)
    ]
    for k in range(chunks):
        part = slice(k * LANES, (k + 1) * LANES)
        c_tiles[pl.ds(k, L, stride=SUB), :] = c_fore[:, part].astype(F32)
        c_tiles[pl.ds(chunks + k, L, stride=SUB), :] = c_back[:, part].astype(F32)
    z_all = jnp.dot(normed[0 : 2 * L], w_in[1], preferred_element_type=F32).astype(BF16)
    z_gate[...] = silu(z_all.astype(F32))
    for copy in shares:
        copy.wait_recv()
    bc = bc_send[...].astype(F32)
    for d in range(1, C):
        bc = bc + bc_recv[d].astype(F32)
    b_fore = bc[0:N] / keep_fore
    r_fore = bc[N : 2 * N] * keep_fore
    b_back = bc[2 * N : 3 * N] / keep_back
    r_back = bc[3 * N :] * keep_back
    for k in range(SUB):
        b_tiles[pl.ds(k, N, stride=SUB), :] = b_fore if k < chunks else b_back
        r_tiles[pl.ds(k, N, stride=SUB), :] = r_fore if k < chunks else r_back

    upper = lax.broadcasted_iota(jnp.int32, (SUB, LANES), 0) < chunks

    def tile(ref, n):
        return ref[pl.ds(n * SUB, SUB), :]

    def across(ref, n, s):
        return jnp.broadcast_to(tile(ref, n)[:, s : s + 1], (SUB, LANES))

    def turn_lanes(ref):
        for n in range(N):
            ref[pl.ds(n * SUB, SUB), :] = pltpu.roll(tile(ref, n), LANES - PER_TURN, 1)

    def step_rows(j):
        fore = pl.multiple_of(j * SUB, SUB)
        back = pl.multiple_of((L - 1 - j) * SUB, SUB)
        return fore, back

    def local_turn(i, states):
        states = list(states)
        for s in range(PER_TURN):
            fore, back = step_rows(i * PER_TURN + s)
            x = jnp.where(upper, c_tiles[pl.ds(fore, SUB), :], c_tiles[pl.ds(back, SUB), :])
            y = jnp.zeros((SUB, LANES), F32)
            for n in range(N):
                states[n] = tile(a_tiles, n) * states[n] + across(b_tiles, n, s) * x
                y = y + across(r_tiles, n, s) * (tile(g_tiles, n) * states[n])
            y_tiles[pl.ds(fore, chunks), :] = y[0:chunks]
            y_tiles[pl.ds(back + chunks, chunks), :] = y[chunks:]
        turn_lanes(b_tiles)
        turn_lanes(r_tiles)
        return tuple(states)

    zeros = tuple(jnp.zeros((SUB, LANES), F32) for _ in range(N))
    states = lax.fori_loop(0, L // PER_TURN, local_turn, zeros)

    own_keep = block_keep[pl.ds(seq, 1), :]
    for n in range(N):
        end_send[n] = own_keep * states[n]
    ends = []
    for d in range(1, S):
        to = at_seq(d)
        mine = pl.ds(lax.rem(to, Q) * per_owner, per_owner)
        ends.append(
            send(end_send.at[mine], end_recv.at[seq], end_s.at[d], end_r.at[d], (to, ch))
        )
    own_n = pl.ds(own_slot * per_owner, per_owner)
    end_recv[seq] = end_send[own_n]
    for copy in ends:
        copy.wait_recv()
    tile_rows = pl.ds(pl.multiple_of(own_slot * per_owner * SUB, SUB), per_owner * SUB)
    block_decay = a_tiles[tile_rows, :]
    for _ in range(L.bit_length() - 1):
        block_decay = block_decay * block_decay
    block_decay = block_decay.reshape(per_owner, SUB, LANES)
    value = jnp.zeros((per_owner, SUB, LANES), F32)
    for s in range(S):
        far = S - 1 - s
        start_send[s, :, 0:chunks] = value[:, 0:chunks]
        start_send[far, :, chunks:] = value[:, chunks:]
        ended = jnp.where(upper, end_recv[s], end_recv[far])
        kept = jnp.where(upper, block_keep[s : s + 1, :], block_keep[far : far + 1, :])
        value = ended + kept * block_decay * value
    starts = []
    for d in range(1, Q):
        to = half * Q + lax.rem(own_slot + d, Q)
        starts.append(
            send(start_send.at[to], start_recv.at[own_slot], start_s.at[d], start_r.at[d], (to, ch))
        )
    start_recv[own_slot] = start_send[seq]
    for copy in starts:
        copy.wait_recv()

    entering = []
    for n in range(N):
        entering.append(tile(g_tiles, n) * start_recv[n // per_owner, n % per_owner])

    def entering_turn(i, states):
        states = list(states)
        for s in range(PER_TURN):
            fore, back = step_rows(i * PER_TURN + s)
            y = jnp.zeros((SUB, LANES), F32)
            for n in range(N):
                states[n] = tile(a_tiles, n) * states[n]
                y = y + across(r_tiles, n, s) * states[n]
            here = pl.ds(fore, chunks)
            there = pl.ds(back + chunks, chunks)
            y_tiles[here, :] = y_tiles[here, :] + y[0:chunks]
            y_tiles[there, :] = y_tiles[there, :] + y[chunks:]
        turn_lanes(r_tiles)
        return tuple(states)

    lax.fori_loop(0, L // PER_TURN, entering_turn, tuple(entering))

    for k in range(2 * chunks):
        part = slice((k % chunks) * LANES, (k % chunks + 1) * LANES)
        at = pl.ds(k, L, stride=SUB)
        row = (k // chunks) * L
        y = y_tiles[at, :] + skip[0:1, part] * c_tiles[at, :]
        y_both[:, k * LANES : (k + 1) * LANES] = (y * z_gate[row : row + L, part]).astype(BF16)

    sums = []
    for d in range(1, C):
        out_send[d] = jnp.dot(y_both[...], w_cat[at_ch(d)], preferred_element_type=F32).astype(BF16)
        sums.append(
            send(out_send.at[d], out_recv.at[d], out_s.at[d], out_r.at[d], (seq, at_ch(d)))
        )
    total = jnp.dot(y_both[...], w_cat[ch], preferred_element_type=F32)
    for d, copy in enumerate(sums):
        copy.wait_recv()
        total = total + out_recv[d + 1].astype(F32)
    out_ref[...] = total.astype(BF16)

    for copy in gathers + halos + shares + ends + starts + sums:
        copy.wait_send()


def solution(mesh):
    S, C = mesh.shape["seq"], mesh.shape["ch"]

    def body(
        hidden, tokens, edit_bounds, norm_gain, base_embed, w_in, conv_w, conv_b, proj_bc, decay_rate, skip_gain, w_out
    ):
        L, width = hidden.shape
        N, inner = decay_rate.shape
        D = C * width
        Q = S // 2
        per_owner = N // Q
        any_space = pl.BlockSpec(memory_space=pl.ANY)
        vmem = pltpu.VMEM
        dma = pltpu.SemaphoreType.DMA
        return pl.pallas_call(
            functools.partial(layer_kernel, S, C, L, N),
            out_shape=jax.ShapeDtypeStruct((L, width), BF16),
            in_specs=[any_space, pl.BlockSpec(memory_space=pltpu.SMEM)] + [any_space] * 10,
            out_specs=pl.BlockSpec(memory_space=pltpu.VMEM),
            scratch_shapes=[
                vmem((S, L), jnp.int32), vmem((1, D), F32), vmem((4, D), F32),
                vmem((2, D, inner), BF16), vmem((CONV, inner), F32), vmem((1, inner), F32),
                vmem((2 * N, inner), BF16), vmem((N, inner), F32), vmem((1, inner), F32),
                vmem((C, 2 * inner, width), BF16),
                vmem((C, L, width), BF16), vmem((C, HALO, width), BF16), vmem((C, HALO, width), BF16),
                vmem((2 * L + 2 * HALO, D), BF16),
                vmem((L + HALO, inner), F32), vmem((L + HALO, inner), F32), vmem((2 * L, inner), F32),
                vmem((L * SUB, LANES), F32), vmem((L * SUB, LANES), F32),
                vmem((4 * N, LANES), BF16), vmem((C, 4 * N, LANES), BF16),
                vmem((N * SUB, LANES), F32), vmem((N * SUB, LANES), F32),
                vmem((N * SUB, LANES), F32), vmem((N * SUB, LANES), F32), vmem((S, LANES), F32),
                vmem((N, SUB, LANES), F32), vmem((S, per_owner, SUB, LANES), F32),
                vmem((S, per_owner, SUB, LANES), F32), vmem((Q, per_owner, SUB, LANES), F32),
                vmem((L, 2 * inner), BF16), vmem((C, L, width), BF16), vmem((C, L, width), BF16),
                dma((11 + C,)), dma((C,)), dma((C,)), dma((C,)), dma((C,)), dma((C,)), dma((C,)),
                dma((C,)), dma((C,)), dma((S,)), dma((S,)), dma((Q,)), dma((Q,)), dma((C,)), dma((C,)),
            ],
            compiler_params=pltpu.CompilerParams(
                collective_id=0, has_side_effects=True, vmem_limit_bytes=60 * 1024 * 1024
            ),
            name="layer",
        )(
            tokens.reshape(S, L), edit_bounds.T, hidden, norm_gain.reshape(1, D), base_embed, w_in,
            conv_w, conv_b.reshape(1, inner), proj_bc, decay_rate, skip_gain.reshape(1, inner), w_out,
        )

    placed = (
        P("seq", "ch"), P(), P(), P(), P(), P(None, None, "ch"), P(None, "ch"), P("ch"),
        P(None, "ch"), P(None, "ch"), P("ch"), P("ch", None),
    )
    return jax.shard_map(
        body, mesh=mesh, in_specs=placed, out_specs=P("seq", "ch"), check_vma=False
    )
```

```python
import functools

import jax
import jax.numpy as jnp
from jax import lax
from jax.experimental import pallas as pl
from jax.experimental.pallas import tpu as pltpu
from jax.sharding import PartitionSpec as P

MESH = pl.DeviceIdType.MESH
F32 = jnp.float32
BF16 = jnp.bfloat16
CONV = 4
REGION = 4
EPSILON = 1e-05
HALO = 8
SUB = 8
LANES = 128
PER_TURN = 16
EARLY_TURNS = 6


def exchange(width, dtype):
    row = lax.broadcasted_iota(jnp.int32, (width, width), 0)
    col = lax.broadcasted_iota(jnp.int32, (width, width), 1)
    return (row + col == width - 1).astype(F32).astype(dtype)


def one_minus_exp(x):
    series = jnp.ones_like(x)
    for order in range(11, 1, -1):
        series = 1.0 - series * x * (1.0 / order)
    return jnp.where(x < 0.5, series * x, 1.0 - jnp.exp(-x))


def silu(x):
    return x * jax.nn.sigmoid(x)


def layer_kernel(
    S, C, L, N,
    tokens_h, bounds, hidden_h, gain_h, embed_h, w_in_h, conv_w_h, conv_b_h, proj_h, rate_h, skip_h, w_out_h,
    out_ref,
    tokens, gain, embed, w_in, conv_w, conv_b, proj, rate, skip, w_cat,
    rows_in, prev_in, next_in, normed,
    x_fore, x_back, z_gate, c_rows, c_tiles, y_tiles,
    bc_send, bc_recv, b_lanes, b_tiles, r_tiles, decay_rows, a_tiles, g_tiles, block_keep, block_decay,
    end_send, end_recv, start_send, start_recv, v_tiles, t_tiles,
    y_both, out_send, out_recv,
    local_sem, gather_s, gather_r, prev_s, prev_r, next_s, next_r,
    bc_s, bc_r, end_s, end_r, near_s, near_r, start_s, start_r, out_s, out_r,
):
    seq = lax.axis_index("seq")
    ch = lax.axis_index("ch")
    region = seq // REGION
    member = lax.rem(seq, REGION)
    width = hidden_h.shape[1]
    inner = w_in.shape[2]
    chunks = inner // LANES

    def at_seq(offset):
        return lax.rem(seq + offset + S, S)

    def at_ch(offset):
        return lax.rem(ch + offset + C, C)

    fetched = [
        (tokens_h, tokens), (gain_h, gain), (embed_h, embed), (conv_w_h, conv_w), (conv_b_h, conv_b),
        (proj_h, proj), (rate_h, rate), (skip_h, skip), (hidden_h, rows_in.at[ch]),
        (w_in_h.at[0], w_in.at[0]), (w_in_h.at[1], w_in.at[1]),
    ]
    fetched += [
        (w_out_h.at[:, pl.ds(k * width, width)], w_cat.at[k, pl.ds(0, inner)]) for k in range(C)
    ]
    local = [
        pltpu.make_async_copy(src, dst, local_sem.at[k]) for k, (src, dst) in enumerate(fetched)
    ]
    for copy in local:
        copy.start()

    barrier = pltpu.get_barrier_semaphore()
    partners = [(seq, at_ch(d)) for d in range(1, C)]
    partners += [(at_seq(side), at_ch(d)) for side in (1, -1) for d in range(C)]
    partners += [(at_seq(d), ch) for d in range(2, S - 1)]
    for partner in partners:
        pl.semaphore_signal(barrier, inc=1, device_id=partner, device_id_type=MESH)
    pl.semaphore_wait(barrier, len(partners))

    def send(src, dst, send_sem, recv_sem, where):
        copy = pltpu.make_async_remote_copy(
            src_ref=src, dst_ref=dst, send_sem=send_sem, recv_sem=recv_sem,
            device_id=where, device_id_type=MESH,
        )
        copy.start()
        return copy

    gathers = [
        send(hidden_h, rows_in.at[ch], gather_s.at[d], gather_r.at[d], (seq, at_ch(d)))
        for d in range(1, C)
    ]
    halos = []
    for d in range(C):
        halos.append(
            send(
                hidden_h.at[pl.ds(L - HALO, HALO)], prev_in.at[ch], prev_s.at[d], prev_r.at[d],
                (at_seq(1), at_ch(d)),
            )
        )
        halos.append(
            send(
                hidden_h.at[pl.ds(0, HALO)], next_in.at[ch], next_s.at[d], next_r.at[d],
                (at_seq(-1), at_ch(d)),
            )
        )

    for copy in local:
        copy.wait()

    flip = exchange(width, BF16)
    flip_lanes = exchange(LANES, BF16)
    for k in range(C):
        w_cat[k, pl.ds(inner, inner)] = jnp.dot(
            w_cat[C - 1 - k, pl.ds(0, inner)], flip, preferred_element_type=F32
        ).astype(BF16)
    decay = jnp.exp(-rate[...])
    drive = jnp.sqrt(one_minus_exp(2.0 * rate[...]))
    decay_rows[...] = decay
    long_decay = decay
    for _ in range(L.bit_length() - 1):
        long_decay = long_decay * long_decay
    for k in range(chunks):
        block_decay[k] = long_decay[:, k * LANES : (k + 1) * LANES]
    for k in range(SUB):
        part = slice((k % chunks) * LANES, (k % chunks + 1) * LANES)
        a_tiles[pl.ds(k, N, stride=SUB), :] = decay[:, part]
        g_tiles[pl.ds(k, N, stride=SUB), :] = drive[:, part]

    def keep_at(places):
        hits = jnp.zeros(places.shape, F32)
        for i in range(bounds.shape[0]):
            for j in range(bounds.shape[1]):
                hits = hits + (places == bounds[i, j]).astype(F32)
        return 1.0 / (1.0 + hits)

    lane = lax.broadcasted_iota(jnp.int32, (S, LANES), 1)
    kept = keep_at(lax.broadcasted_iota(jnp.int32, (S, LANES), 0) * L + lane)
    shift = LANES // 2
    while shift:
        kept = kept * pltpu.roll(kept, shift, 1)
        shift //= 2
    block_keep[...] = kept

    lane_row = lax.broadcasted_iota(jnp.int32, (SUB, LANES), 1)

    def running_keep(places):
        run = keep_at(places)
        step = 1
        while step < LANES:
            run = run * jnp.where(lane_row >= step, pltpu.roll(run, step, 1), 1.0)
            step *= 2
        return run[0:1]

    keep_fore = running_keep(seq * L + lane_row)
    keep_back = running_keep(seq * L + (L - 1) - lane_row)

    def base_of(block):
        row = tokens[pl.ds(block, 1), :].astype(F32)
        return jnp.broadcast_to(row, (LANES, LANES)).T[:, 0:1]

    own_base = base_of(seq)
    prev_base = base_of(at_seq(-1))[L - HALO :]
    next_base = base_of(at_seq(1))[:HALO]

    for copy in gathers:
        copy.wait_recv()
    for copy in halos:
        copy.wait_recv()

    def norm_into(block, base, emit):
        total = jnp.zeros((block.shape[1], 1), F32)
        for k in range(C):
            part = block[k].astype(F32)
            total = total + jnp.sum(part * part, axis=1, keepdims=True)
        inv_rms = lax.rsqrt(total * (1.0 / (C * width)) + EPSILON)
        for k in range(C):
            cols = slice(k * width, (k + 1) * width)
            added = jnp.where(base == 0.0, embed[0:1, cols], embed[1:2, cols])
            added = jnp.where(base == 2.0, embed[2:3, cols], added)
            added = jnp.where(base == 3.0, embed[3:4, cols], added)
            emit(k, (block[k].astype(F32) * inv_rms * gain[0:1, cols] + added).astype(BF16))

    def flipped(part):
        return jnp.dot(part, flip, preferred_element_type=F32).astype(BF16)

    def emit_own(k, part):
        normed[0:L, k * width : (k + 1) * width] = part
        k = C - 1 - k
        normed[L : 2 * L, k * width : (k + 1) * width] = flipped(part)

    edge_prev = []
    edge_next = []
    norm_into(rows_in, own_base, emit_own)
    norm_into(prev_in, prev_base, lambda k, part: edge_prev.append(part))
    norm_into(next_in, next_base, lambda k, part: edge_next.append(part))
    for k in range(C):
        both = jnp.concatenate([edge_prev[k], edge_next[k]], axis=0)
        turned = flipped(jnp.concatenate([edge_prev[C - 1 - k], edge_next[C - 1 - k]], axis=0))
        top = lax.broadcasted_iota(jnp.int32, both.shape, 0) < HALO
        normed[2 * L :, k * width : (k + 1) * width] = jnp.where(top, both, turned)

    x_all = jnp.dot(normed[...], w_in[0], preferred_element_type=F32).astype(BF16).astype(F32)
    has_prev = jnp.where(seq > 0, 1.0, 0.0)
    has_next = jnp.where(seq < S - 1, 1.0, 0.0)
    x_fore[0:HALO] = x_all[2 * L : 2 * L + HALO] * has_prev
    x_fore[HALO:] = x_all[0:L]
    x_back[0:L] = x_all[L : 2 * L]
    x_back[L:] = x_all[2 * L + HALO :] * has_next
    sum_fore = jnp.broadcast_to(conv_b[...], (L, inner))
    sum_back = sum_fore
    for k in range(CONV):
        tap = conv_w[k : k + 1, :]
        sum_fore = sum_fore + x_fore[pl.ds(HALO - CONV + 1 + k, L), :] * tap
        sum_back = sum_back + x_back[pl.ds(CONV - 1 - k, L), :] * tap
    c_fore = silu(sum_fore).astype(BF16)
    c_back = silu(sum_back).astype(BF16)

    nt = (((1,), (1,)), ((), ()))
    part_fore = lax.dot_general(proj[...], c_fore, nt, preferred_element_type=F32).astype(BF16)
    part_back = lax.dot_general(proj[...], c_back, nt, preferred_element_type=F32).astype(BF16)
    bc_send[0 : 2 * N] = part_fore
    bc_send[2 * N :] = jnp.dot(part_back, flip_lanes, preferred_element_type=F32).astype(BF16)
    shares = [
        send(bc_send, bc_recv.at[d], bc_s.at[d], bc_r.at[d], (seq, at_ch(d))) for d in range(1, C)
    ]
    for k in range(chunks):
        part = slice(k * LANES, (k + 1) * LANES)
        c_rows[k] = c_fore[:, part].astype(F32)
        c_rows[chunks + k] = c_back[:, part].astype(F32)
        c_tiles[pl.ds(k, L, stride=SUB), :] = c_fore[:, part].astype(F32)
        c_tiles[pl.ds(chunks + k, L, stride=SUB), :] = c_back[:, part].astype(F32)
    z_all = jnp.dot(normed[0 : 2 * L], w_in[1], preferred_element_type=F32).astype(BF16)
    z_gate[...] = silu(z_all.astype(F32))
    for copy in shares:
        copy.wait_recv()
    bc = bc_send[...].astype(F32)
    for d in range(1, C):
        bc = bc + bc_recv[d].astype(F32)
    b_fore = bc[0:N] / keep_fore
    r_fore = bc[N : 2 * N] * keep_fore
    b_back = bc[2 * N : 3 * N] / keep_back
    r_back = bc[3 * N :] * keep_back
    b_lanes[0] = b_fore
    b_lanes[1] = b_back
    for k in range(SUB):
        b_tiles[pl.ds(k, N, stride=SUB), :] = b_fore if k < chunks else b_back
        r_tiles[pl.ds(k, N, stride=SUB), :] = r_fore if k < chunks else r_back

    def end_turn(i, states):
        states = list(states)
        for s in range(PER_TURN):
            at = i * PER_TURN + s
            for way in range(2):
                row = at if way == 0 else L - 1 - at
                b = b_lanes[way]
                b = [
                    jnp.broadcast_to(b[h * SUB : (h + 1) * SUB, s : s + 1], (SUB, LANES))
                    for h in range(N // SUB)
                ]
                for k in range(chunks):
                    part = pl.ds(k * LANES, LANES)
                    x = c_rows[way * chunks + k, pl.ds(row, SUB, stride=0), :]
                    for h in range(N // SUB):
                        slot = (way * chunks + k) * (N // SUB) + h
                        states[slot] = decay_rows[pl.ds(h * SUB, SUB), part] * states[slot] + b[h] * x
        for way in range(2):
            b_lanes[way] = pltpu.roll(b_lanes[way], LANES - PER_TURN, 1)
        return tuple(states)

    zeros = tuple(jnp.zeros((SUB, LANES), F32) for _ in range(N))
    ended = lax.fori_loop(0, L // PER_TURN, end_turn, zeros)
    own_keep = block_keep[pl.ds(seq, 1), :]
    for way in range(2):
        for k in range(chunks):
            slot = (way * chunks + k) * (N // SUB)
            whole = jnp.concatenate(ended[slot : slot + N // SUB], axis=0)
            end_send[way, k] = (own_keep * whole).astype(BF16)

    ends = []
    for d in range(1, S):
        to = at_seq(d)
        way = jnp.where(to // REGION < region, 1, 0)
        ends.append(
            send(
                end_send.at[way, lax.rem(to, REGION)], end_recv.at[way, seq], end_s.at[d], end_r.at[d],
                (to, ch),
            )
        )
    for d in range(1, REGION):
        to_member = lax.rem(member + d, REGION)
        ends.append(
            send(
                end_send.at[1, to_member], end_recv.at[1, seq], near_s.at[d], near_r.at[d],
                (region * REGION + to_member, ch),
            )
        )
    for way in range(2):
        end_recv[way, seq] = end_send[way, member]

    upper = lax.broadcasted_iota(jnp.int32, (SUB, LANES), 0) < chunks

    def tile(ref, n):
        return ref[pl.ds(n * SUB, SUB), :]

    def across(ref, n, s):
        return jnp.broadcast_to(tile(ref, n)[:, s : s + 1], (SUB, LANES))

    def turn_lanes(ref):
        for n in range(N):
            ref[pl.ds(n * SUB, SUB), :] = pltpu.roll(tile(ref, n), LANES - PER_TURN, 1)

    def tile_rows(j):
        return pl.ds(pl.multiple_of(j * SUB, SUB), SUB)

    for n in range(N):
        v_tiles[pl.ds(n * SUB, SUB), :] = tile(a_tiles, n) * tile(g_tiles, n)

    def local_turn(i, states):
        states = list(states)
        for s in range(PER_TURN):
            j = i * PER_TURN + s
            x = jnp.where(upper, c_tiles[tile_rows(j), :], c_tiles[tile_rows(L - 1 - j), :])
            y = skip_tile * x
            for n in range(N):
                states[n] = tile(a_tiles, n) * states[n] + across(b_tiles, n, s) * x
                r = across(r_tiles, n, s)
                y = y + r * (tile(g_tiles, n) * states[n])
                reach = tile(v_tiles, n)
                t_tiles[j * N + n] = r * reach
                v_tiles[pl.ds(n * SUB, SUB), :] = reach * tile(a_tiles, n)
            y_tiles[tile_rows(j), :] = y
        turn_lanes(b_tiles)
        turn_lanes(r_tiles)
        return tuple(states)

    skip_tile = jnp.concatenate(
        [skip[0:1, (k % chunks) * LANES : (k % chunks + 1) * LANES] for k in range(SUB)], axis=0
    )
    turns = L // PER_TURN
    states = lax.fori_loop(0, EARLY_TURNS, local_turn, zeros)

    for copy in ends:
        copy.wait_recv()
    decay_here = block_decay[member]

    def carry_on(way, i, value):
        factor = block_keep[pl.ds(i, 1), :] * decay_here
        return end_recv[way, i].astype(F32) + factor * value

    def fore_region(g, value):
        for k in range(REGION):
            value = carry_on(0, g * REGION + k, value)
        return value

    def back_region(g, value):
        for k in range(REGION):
            value = carry_on(1, S - 1 - (g * REGION + k), value)
        return value

    value = lax.fori_loop(0, region, fore_region, jnp.zeros((N, LANES), F32))
    for k in range(REGION):
        start_send[k, 0] = value.astype(BF16)
        value = carry_on(0, region * REGION + k, value)
    value = lax.fori_loop(0, S // REGION - 1 - region, back_region, jnp.zeros((N, LANES), F32))
    for k in range(REGION - 1, -1, -1):
        start_send[k, 1] = value.astype(BF16)
        value = carry_on(1, region * REGION + k, value)
    starts = []
    for d in range(1, REGION):
        to_member = lax.rem(member + d, REGION)
        starts.append(
            send(
                start_send.at[to_member], start_recv.at[member], start_s.at[d], start_r.at[d],
                (region * REGION + to_member, ch),
            )
        )
    start_recv[member] = start_send[member]
    lax.fori_loop(EARLY_TURNS, turns, local_turn, states)
    for copy in starts:
        copy.wait_recv()

    for k in range(SUB):
        v_tiles[pl.ds(k, N, stride=SUB), :] = start_recv[k % chunks, k // chunks].astype(F32)
    entering = [tile(v_tiles, n) for n in range(N)]

    def entering_turn(i, carried):
        for s in range(SUB):
            j = i * SUB + s
            parts = [t_tiles[j * N + n] * entering[n] for n in range(N)]
            while len(parts) > 1:
                parts = [parts[k] + parts[k + 1] for k in range(0, len(parts), 2)]
            y = y_tiles[tile_rows(j), :] + parts[0]
            c_tiles[pl.ds(pl.multiple_of(j * SUB, SUB), chunks), :] = y[0:chunks]
            there = pl.multiple_of((L - 1 - j) * SUB, SUB) + chunks
            c_tiles[pl.ds(there, chunks), :] = y[chunks:]
        return carried

    lax.fori_loop(0, L // SUB, entering_turn, 0)

    for k in range(2 * chunks):
        part = slice((k % chunks) * LANES, (k % chunks + 1) * LANES)
        row = (k // chunks) * L
        y = c_tiles[pl.ds(k, L, stride=SUB), :] * z_gate[row : row + L, part]
        y_both[:, k * LANES : (k + 1) * LANES] = y.astype(BF16)

    sums = []
    for d in range(1, C):
        out_send[d] = jnp.dot(y_both[...], w_cat[at_ch(d)], preferred_element_type=F32).astype(BF16)
        sums.append(
            send(out_send.at[d], out_recv.at[d], out_s.at[d], out_r.at[d], (seq, at_ch(d)))
        )
    total = jnp.dot(y_both[...], w_cat[ch], preferred_element_type=F32)
    for d, copy in enumerate(sums):
        copy.wait_recv()
        total = total + out_recv[d + 1].astype(F32)
    out_ref[...] = total.astype(BF16)

    for copy in gathers + halos + shares + ends + starts + sums:
        copy.wait_send()


def solution(mesh):
    S, C = mesh.shape["seq"], mesh.shape["ch"]

    def body(
        hidden, tokens, edit_bounds, norm_gain, base_embed, w_in, conv_w, conv_b, proj_bc, decay_rate, skip_gain, w_out
    ):
        L, width = hidden.shape
        N, inner = decay_rate.shape
        D = C * width
        chunks = inner // LANES
        any_space = pl.BlockSpec(memory_space=pl.ANY)
        vmem = pltpu.VMEM
        dma = pltpu.SemaphoreType.DMA
        return pl.pallas_call(
            functools.partial(layer_kernel, S, C, L, N),
            out_shape=jax.ShapeDtypeStruct((L, width), BF16),
            in_specs=[any_space, pl.BlockSpec(memory_space=pltpu.SMEM)] + [any_space] * 10,
            out_specs=pl.BlockSpec(memory_space=pltpu.VMEM),
            scratch_shapes=[
                vmem((S, L), jnp.int32), vmem((1, D), F32), vmem((4, D), F32),
                vmem((2, D, inner), BF16), vmem((CONV, inner), F32), vmem((1, inner), F32),
                vmem((2 * N, inner), BF16), vmem((N, inner), F32), vmem((1, inner), F32),
                vmem((C, 2 * inner, width), BF16),
                vmem((C, L, width), BF16), vmem((C, HALO, width), BF16), vmem((C, HALO, width), BF16),
                vmem((2 * L + 2 * HALO, D), BF16),
                vmem((L + HALO, inner), F32), vmem((L + HALO, inner), F32), vmem((2 * L, inner), F32),
                vmem((2 * chunks, L, LANES), F32), vmem((L * SUB, LANES), F32), vmem((L * SUB, LANES), F32),
                vmem((4 * N, LANES), BF16), vmem((C, 4 * N, LANES), BF16),
                vmem((2, N, LANES), F32), vmem((N * SUB, LANES), F32), vmem((N * SUB, LANES), F32),
                vmem((N, inner), F32), vmem((N * SUB, LANES), F32), vmem((N * SUB, LANES), F32),
                vmem((S, LANES), F32), vmem((chunks, N, LANES), F32),
                vmem((2, chunks, N, LANES), BF16), vmem((2, S, N, LANES), BF16),
                vmem((REGION, 2, N, LANES), BF16), vmem((REGION, 2, N, LANES), BF16),
                vmem((N * SUB, LANES), F32), vmem((L * N, SUB, LANES), F32),
                vmem((L, 2 * inner), BF16), vmem((C, L, width), BF16), vmem((C, L, width), BF16),
                dma((11 + C,)), dma((C,)), dma((C,)), dma((C,)), dma((C,)), dma((C,)), dma((C,)),
                dma((C,)), dma((C,)), dma((S,)), dma((S,)), dma((REGION,)), dma((REGION,)),
                dma((REGION,)), dma((REGION,)), dma((C,)), dma((C,)),
            ],
            compiler_params=pltpu.CompilerParams(
                collective_id=0, has_side_effects=True, vmem_limit_bytes=60 * 1024 * 1024
            ),
            name="layer",
        )(
            tokens.reshape(S, L), edit_bounds.T, hidden, norm_gain.reshape(1, D), base_embed, w_in,
            conv_w, conv_b.reshape(1, inner), proj_bc, decay_rate, skip_gain.reshape(1, inner), w_out,
        )

    placed = (
        P("seq", "ch"), P(), P(), P(), P(), P(None, None, "ch"), P(None, "ch"), P("ch"),
        P(None, "ch"), P(None, "ch"), P("ch"), P("ch", None),
    )
    return jax.shard_map(
        body, mesh=mesh, in_specs=placed, out_specs=P("seq", "ch"), check_vma=False
    )
```
